256 devices in a mesh: expert: 64 (over z, x, core), tensor: 4 (over y).
Axes of the slice: x: 4, y: 4, z: 8, core: 2. Of those that a mesh axis runs over, the one named last changes fastest.
Arguments:
- tokens: bfloat16 [16384, 2048], P('expert', 'tensor'), may hold values from -6 to 6
- out_grads: bfloat16 [16384, 2048], P('expert', 'tensor'), may hold values from -6 to 6
- species: int32 [16384, 1], P('expert'), may hold values from 0 to 63; in each aligned block of 64 rows (0 to 63, 64 to 127, ...) at most 2 rows name the same one
- expert_table: int32 [64], replicated, may hold values from 0 to 63, each once
- gate_weight: bfloat16 [64, 2048, 4096], P('expert', None, 'tensor'), may hold values from -0.125 to 0.125
- up_weight: bfloat16 [64, 2048, 4096], P('expert', None, 'tensor'), may hold values from -0.125 to 0.125
- down_weight: bfloat16 [64, 4096, 2048], P('expert', 'tensor'), may hold values from -0.09375 to 0.09375
Outputs:
- token_grads: bfloat16 [16384, 2048], P('expert', 'tensor')
The draws below stay inside these ranges and needn't reach their ends.
Inputs may be any that keep to these rules, and one draw needn't show every extreme that they name: In each aligned block of 64 rows no species occurs more than 2 times, and in some blocks one species occurs exactly 2 times. `expert_table`: each species has a different expert.
All inputs are finite; a program needn't handle non-finite values.
Results may differ from the reference program's by a relative error of at most 0.0095.
Values may be sent and summed in bfloat16 or wider, within the bound.
A program may use at most 64 MiB of HBM per device.

```python
import math
import jax
import jax.numpy as jnp
import numpy as np
from jax import lax

D = 2048
FF = 4096
EXPERTS = 64
TOKENS = 16384
ROWS_DEV = 64
FF_DEV = 1024
CAP = 2
SLOTS = 512
N_TENSOR = 4


def block_levels(rng, shape, pieces, low, high):
    def one(dim, parts):
        steps = jax.random.uniform(jax.random.fold_in(jax.random.fold_in(rng, 6), dim), (parts,), jnp.float32, low / len(pieces), high / len(pieces))
        return jnp.repeat(jnp.exp(steps), shape[dim] // parts).reshape((-1,) + (1,) * (len(shape) - dim - 1))

    factor_of = one(*pieces[0])
    for cut in pieces[1:]:
        factor_of = factor_of * one(*cut)
    return factor_of


def assign_block(rng, own, number, rows, number_of, top, most, lean):
    order = jax.random.permutation(rng, number_of)
    crowded, ordinary = shares(number_of, rows * top, most, lean, True), shares(number_of, rows * top, most, lean, False)
    places = jnp.arange(number_of)

    def named(sizes, rotation):
        used = int((sizes > 0).sum())
        fixed = max(1, used // 4)
        passed = fixed + (places - fixed + rotation * (used - fixed)) % max(1, number_of - fixed)
        return jnp.zeros((number_of,), jnp.int32).at[order[jnp.where(places < fixed, places, passed)]].set(jnp.asarray(sizes, jnp.int32))

    sizes = jnp.where(number % 4 == 0, named(crowded, number // 4), named(ordinary, number - number // 4 - 1))
    mixed = jax.random.permutation(jax.random.fold_in(own, 3), number_of)
    source_of, receiver = mixed[0:number_of // 2 * 2:2], mixed[1:number_of // 2 * 2:2]
    margin = jnp.minimum(sizes[source_of] - 1, most - sizes[receiver]) // 2
    margin = jnp.where((source_of == order[0]) | (receiver == order[0]) | (sizes[receiver] == 0), 0, jnp.maximum(margin, 0))
    passed = jax.random.randint(jax.random.fold_in(own, 4), (number_of // 2,), 0, 1 << 20) % (margin + 1)
    sizes = sizes.at[source_of].add(-passed).at[receiver].add(passed)
    items = jnp.searchsorted(jnp.cumsum(sizes), jnp.arange(rows * top), side="right").astype(jnp.int32)
    listing = items.reshape(top, rows).T
    listing = listing[jax.random.permutation(jax.random.fold_in(own, 1), rows)]
    rotation = jax.random.randint(jax.random.fold_in(own, 2), (rows, 1), 0, top)
    return jnp.take_along_axis(listing, (jnp.arange(top)[None, :] + rotation) % top, axis=1)


def shares(number_of, total, most, slope, full):
    loads = [(1 << 20) // math.isqrt(rank ** slope) + 1 for rank in range(1, number_of + 1)]
    largest = most if full else min(most, max(-(-total // number_of), total * loads[0] // sum(loads)))
    least = 1 if total - largest >= number_of - 1 else 0
    holding, rest = [largest] + [least] * (number_of - 1), total - largest - least * (number_of - 1)
    while rest > 0:
        candidates = [i for i in range(1, number_of) if holding[i] < largest] or [i for i in range(1, number_of) if holding[i] < most]
        pool, left = sum([loads[i] for i in candidates]), rest
        for i in candidates:
            more = min(most - holding[i], max(1, left * loads[i] // pool), rest)
            holding[i] = holding[i] + more
            rest = rest - more
    return np.array(holding)


def bell_draw(own_key, extent, width, reach, split=(), kind=jnp.bfloat16):
    result = jax.random.normal(own_key, extent, jnp.float32) * width
    if len(split) > 0:
        result = block_levels(own_key, extent, split, -0.22, 0.18) * result
    return jnp.clip(result, min=-reach, max=reach).astype(kind)


def setup_inputs(seed: int = 0) -> dict:
    seeds = jax.random.split(jax.random.key(seed), 8)
    tokens = bell_draw(seeds[0], (TOKENS, D), 1.0, 6.0, ((0, 64), (1, 4)))
    out_grads = bell_draw(seeds[1], (TOKENS, D), 1.0, 6.0, ((0, 64), (1, 4)))
    species_keys = jax.random.split(jax.random.fold_in(seeds[2], 1), TOKENS // ROWS_DEV)
    species_turns = jax.random.permutation(jax.random.fold_in(seeds[2], 3), TOKENS // ROWS_DEV)
    species = jax.vmap(lambda own, number: assign_block(jax.random.fold_in(seeds[2], 2), own, number, ROWS_DEV, EXPERTS, 1, CAP, 2))(species_keys, species_turns).reshape((TOKENS, 1))
    expert_table = jax.random.permutation(seeds[3], EXPERTS).astype(jnp.int32)
    gate_weight = bell_draw(seeds[4], (EXPERTS, D, FF), D ** -0.5, 0.125, ((0, 64), (2, 4)))
    up_weight = bell_draw(seeds[5], (EXPERTS, D, FF), D ** -0.5, 0.125, ((0, 64), (2, 4)))
    down_weight = bell_draw(seeds[6], (EXPERTS, FF, D), FF ** -0.5, 0.09375, ((0, 64), (1, 4)))
    return dict(tokens=tokens, out_grads=out_grads, species=species, expert_table=expert_table, gate_weight=gate_weight, up_weight=up_weight, down_weight=down_weight)


def slot_positions(species, expert_table):
    expert_of = expert_table[species[:, 0]].astype(jnp.int32)
    blocked = expert_of.reshape(-1, ROWS_DEV)
    expert_ids = jnp.arange(EXPERTS, dtype=jnp.int32)
    onehot = (blocked[:, :, None] == expert_ids[None, None, :]).astype(jnp.int32)
    earlier = jnp.cumsum(onehot, axis=1) - onehot
    slot_of = jnp.sum(earlier * onehot, axis=2)
    block_ids = jnp.arange(blocked.shape[0], dtype=jnp.int32)[:, None]
    position = blocked * SLOTS + block_ids * CAP + slot_of
    return position.reshape(-1).astype(jnp.int32)


def expert_pass(expert_rows, expert_grads, gate_matrix, up_matrix, down_matrix):
    contract = (((1,), (1,)), ((), ()))
    gate_pre = jnp.dot(expert_rows, gate_matrix, preferred_element_type=jnp.float32)
    up_pre = jnp.dot(expert_rows, up_matrix, preferred_element_type=jnp.float32)
    hidden_grad = lax.dot_general(expert_grads, down_matrix, contract, preferred_element_type=jnp.float32)
    sigmoid_gate = jax.nn.sigmoid(gate_pre)
    up_grad = (hidden_grad * gate_pre * sigmoid_gate).astype(jnp.bfloat16)
    gate_grad = (hidden_grad * up_pre * sigmoid_gate * (1.0 + gate_pre * (1.0 - sigmoid_gate))).astype(jnp.bfloat16)
    running = jnp.zeros((expert_rows.shape[0], D), jnp.float32)
    for block_index in range(N_TENSOR):
        start = block_index * FF_DEV
        partial_sum = lax.dot_general(gate_grad[:, start:start + FF_DEV], gate_matrix[:, start:start + FF_DEV], contract, preferred_element_type=jnp.float32)
        partial_sum = partial_sum + lax.dot_general(up_grad[:, start:start + FF_DEV], up_matrix[:, start:start + FF_DEV], contract, preferred_element_type=jnp.float32)
        rounded = lax.optimization_barrier(partial_sum.astype(jnp.bfloat16))
        running = running + rounded.astype(jnp.float32)
    return running.astype(jnp.bfloat16)


def reference(tokens, out_grads, species, expert_table, gate_weight, up_weight, down_weight):
    position = slot_positions(species, expert_table)
    owner_rows = jnp.full((EXPERTS * SLOTS,), TOKENS, jnp.int32)
    owner_rows = owner_rows.at[position].set(jnp.arange(TOKENS, dtype=jnp.int32))
    owner_rows = owner_rows.reshape(EXPERTS, SLOTS)
    padded_rows = jnp.concatenate([tokens, jnp.zeros((1, D), jnp.bfloat16)], axis=0)
    padded_grads = jnp.concatenate([out_grads, jnp.zeros((1, D), jnp.bfloat16)], axis=0)

    def per_expert(expert_index):
        picked = owner_rows[expert_index]
        return expert_pass(padded_rows[picked], padded_grads[picked], gate_weight[expert_index], up_weight[expert_index], down_weight[expert_index])

    row_grads = lax.map(per_expert, jnp.arange(EXPERTS, dtype=jnp.int32))
    return row_grads.reshape(EXPERTS * SLOTS, D)[position]
```

```python
import functools

import jax
import jax.numpy as jnp
from jax import lax
from jax.experimental import pallas as pl
from jax.experimental.pallas import tpu as pltpu
from jax.sharding import PartitionSpec as P

MESH = pl.DeviceIdType.MESH
F32 = jnp.float32
BF16 = jnp.bfloat16
OFFSETS = (0, 1, -1, 2, -2, 3, -3, 4)
PLANES = 8
MEMBERS = 8
NT = (((1,), (1,)), ((), ()))
TN = (((0,), (0,)), ((), ()))


def place_of(species, table_ref, my_plane, experts, capacity, block):
    count = species.shape[1]
    expert_of = jnp.zeros_like(species)
    for kind in range(experts):
        expert_of = jnp.where(species == kind, table_ref[kind], expert_of)
    ids = lax.broadcasted_iota(jnp.int32, (experts, count), 0)
    hits = ids == expert_of
    before = lax.broadcasted_iota(jnp.int32, (count, count), 0)
    after = lax.broadcasted_iota(jnp.int32, (count, count), 1)
    same_block = (before // block) == (after // block)
    earlier_of = jnp.where((before < after) & same_block, 1.0, 0.0).astype(BF16)
    hits_f = jnp.where(hits, 1.0, 0.0)
    earlier = jnp.dot(hits_f.astype(BF16), earlier_of, preferred_element_type=F32)
    slot = jnp.sum(hits_f * earlier, axis=0, keepdims=True).astype(jnp.int32)
    plane = expert_of // MEMBERS
    away = (plane - my_plane + PLANES) % PLANES
    half = PLANES // 2
    chunk = jnp.where(away == 0, 0, jnp.where(away <= half, 2 * away - 1, 2 * (PLANES - away)))
    chunk = jnp.minimum(chunk, PLANES - 1)
    block_id = lax.broadcasted_iota(jnp.int32, (1, count), 1) // block
    blocks = count // block
    return (chunk * MEMBERS + expert_of % MEMBERS) * (blocks * capacity) + block_id * capacity + slot


def kernel(
    capacity,
    tokens_ref, grads_ref, species_ref, table_ref, gate_hbm, up_hbm, down_hbm,
    out_ref,
    pack, xin, rows, rgrads, gate_w, up_w, down_w, gate_g, up_g,
    send_far, send_near, recv_far, recv_near, sums, ret, select,
    w_sem, a_send, a_recv, y_send, y_recv, o_send, o_recv, f_send, f_recv, n_send, n_recv, r_send, r_recv,
):
    experts = lax.axis_size("expert")
    tensor_size = lax.axis_size("tensor")
    me = lax.axis_index("expert")
    mine = lax.axis_index("tensor")
    my_plane = me // MEMBERS
    my_member = me % MEMBERS
    right = (mine + 1) % tensor_size
    left = (mine + tensor_size - 1) % tensor_size
    width = tokens_ref.shape[1]
    half_slots = experts // 2
    half_rows = half_slots * 8

    feature = (mine, left, right, (mine + 2) % tensor_size)
    weight_copies = []
    for j in range(4):
        start = pl.multiple_of(feature[j] * width, width)
        for w, (src, dst) in enumerate((
            (gate_hbm.at[pl.ds(start, width), :], gate_w.at[pl.ds(j * width, width), :]),
            (up_hbm.at[pl.ds(start, width), :], up_w.at[pl.ds(j * width, width), :]),
            (down_hbm.at[:, pl.ds(start, width)], down_w.at[:, pl.ds(j * width, width)]),
        )):
            copy = pltpu.make_async_copy(src, dst, w_sem.at[w, j])
            copy.start()
            weight_copies.append(copy)

    def device(offset, member):
        plane = (my_plane + offset + PLANES) % PLANES
        return (plane * MEMBERS + member, mine)

    barrier = pltpu.get_barrier_semaphore()
    for c in range(PLANES):
        for r in range(MEMBERS):
            if c == 0 and r == 0:
                continue
            pl.semaphore_signal(barrier, inc=1, device_id=device(OFFSETS[c], (my_member + r) % MEMBERS), device_id_type=MESH)
    for side in (left, right):
        pl.semaphore_signal(barrier, inc=1, device_id=(me, side), device_id_type=MESH)

    block = tokens_ref.shape[0] // tensor_size
    place = place_of(species_ref[...], table_ref, my_plane, experts, capacity, block)
    slot_rows = tensor_size * capacity
    slot_ids = lax.broadcasted_iota(jnp.int32, (experts * slot_rows, place.shape[1]), 0)
    chosen = jnp.where(slot_ids == place, 1.0, 0.0).astype(BF16)
    select[...] = chosen

    def pack_chunk(c):
        part = select[pl.ds(c * 64, 64), :]
        own_rows = jnp.dot(part, tokens_ref[...], preferred_element_type=F32)
        own_grads = jnp.dot(part, grads_ref[...], preferred_element_type=F32)
        both = jnp.concatenate(
            [own_rows.reshape(MEMBERS, 8, width), own_grads.reshape(MEMBERS, 8, width)], axis=1
        )
        pack[pl.ds(c * MEMBERS, MEMBERS)] = both.astype(BF16)

    for c in range(PLANES):
        pack_chunk(c)
    pl.semaphore_wait(barrier, experts - 1 + 2)

    def a_copy(c, member, target):
        return pltpu.make_async_remote_copy(
            src_ref=pack.at[c * MEMBERS + member],
            dst_ref=xin.at[0, c * MEMBERS + my_member],
            send_sem=a_send.at[c],
            recv_sem=a_recv.at[c],
            device_id=target,
            device_id_type=MESH,
        )

    pltpu.make_async_copy(pack.at[my_member], xin.at[0, my_member], a_recv.at[0]).start()
    for c in range(PLANES):
        for r in range(MEMBERS):
            if c == 0 and r == 0:
                continue
            member = (my_member + r) % MEMBERS
            a_copy(c, member, device(OFFSETS[c], member)).start()

    def span(c):
        return pl.ds(c * MEMBERS, MEMBERS)

    def y_copy(side, c):
        return pltpu.make_async_remote_copy(
            src_ref=xin.at[0, span(c)],
            dst_ref=xin.at[1 + side, span(c)],
            send_sem=y_send.at[side, c],
            recv_sem=y_recv.at[side, c],
            device_id=(me, (right, left)[side]),
            device_id_type=MESH,
        )

    def o_copy(side, c):
        part = pl.ds(c * MEMBERS + side * (MEMBERS // 2), MEMBERS // 2)
        return pltpu.make_async_remote_copy(
            src_ref=xin.at[1 + side, part],
            dst_ref=xin.at[3, part],
            send_sem=o_send.at[side, c],
            recv_sem=o_recv.at[side, c],
            device_id=(me, (right, left)[side]),
            device_id_type=MESH,
        )

    def gather_first(c):
        pltpu.make_async_copy(pack.at[span(c)], xin.at[0, span(c)], a_recv.at[c]).wait()
        for side in range(2):
            y_copy(side, c).start()

    def gather_relay(c):
        for side in range(2):
            y_copy(side, c).wait_recv()
            o_copy(side, c).start()

    def gather_last(c):
        for side in range(2):
            o_copy(side, c).wait_recv()

    def unpack_chunks(first, count):
        for j in range(4):
            both = xin[j, pl.ds(first * MEMBERS, count * MEMBERS)].astype(F32)
            at = pl.ds(first * 64, count * 64)
            rows[at, pl.ds(j * width, width)] = both[:, 0:8, :].reshape(count * 64, width).astype(BF16)
            rgrads[at, pl.ds(j * width, width)] = both[:, 8:16, :].reshape(count * 64, width).astype(BF16)

    def forward(h):
        at = pl.ds(h * half_rows, half_rows)

        @pl.loop(0, gate_w.shape[1] // 256)
        def _(n):
            cols = pl.ds(pl.multiple_of(n * 256, 256), 256)
            x = rows[at, :]
            gate = jnp.dot(x, gate_w[:, cols], preferred_element_type=F32)
            up = jnp.dot(x, up_w[:, cols], preferred_element_type=F32)
            hidden = lax.dot_general(rgrads[at, :], down_w[cols, :], NT, preferred_element_type=F32)
            s = jax.nn.sigmoid(gate)
            hs = hidden * s
            up_g[h, :, cols] = (hs * gate).astype(BF16)
            gate_g[h, :, cols] = (hs * up * (1.0 + gate * (1.0 - s))).astype(BF16)

    def partial(h, j):
        feats = pl.ds(j * width, width)
        return lax.dot_general(gate_g[h], gate_w[feats, :], NT, preferred_element_type=F32) + lax.dot_general(
            up_g[h], up_w[feats, :], NT, preferred_element_type=F32
        )

    quarter = half_rows // 2

    def far_copy(side, h):
        return pltpu.make_async_remote_copy(
            src_ref=send_far.at[h, side],
            dst_ref=recv_far.at[h, side],
            send_sem=f_send.at[h, side],
            recv_sem=f_recv.at[h, side],
            device_id=(me, (right, left)[side]),
            device_id_type=MESH,
        )

    def near_copy(side, h):
        return pltpu.make_async_remote_copy(
            src_ref=send_near.at[h, side],
            dst_ref=recv_near.at[h, side],
            send_sem=n_send.at[h, side],
            recv_sem=n_recv.at[h, side],
            device_id=(me, (right, left)[side]),
            device_id_type=MESH,
        )

    def scatter_far(h):
        far = partial(h, 3).astype(BF16)
        for side in range(2):
            send_far[h, side] = far[side * quarter:(side + 1) * quarter]
            far_copy(side, h).start()

    def scatter_near(h):
        for side in range(2):
            near = partial(h, 2 - side)
            far_copy(side, h).wait_recv()
            arrived = recv_far[h, side].astype(F32)
            mid = (near[:quarter], near[quarter:])
            parts = [mid[0], mid[1]]
            parts[side] = parts[side] + arrived
            for i in range(2):
                send_near[h, side, pl.ds(i * quarter, quarter)] = parts[i].astype(BF16)
            near_copy(side, h).start()

    def r_copy(c, member, target):
        return pltpu.make_async_remote_copy(
            src_ref=sums.at[c * MEMBERS + member],
            dst_ref=ret.at[c * MEMBERS + my_member],
            send_sem=r_send.at[c // 4],
            recv_sem=r_recv.at[c // 4],
            device_id=target,
            device_id_type=MESH,
        )

    def scatter_own(h):
        own = partial(h, 0)
        for side in range(2):
            near_copy(side, h).wait_recv()
            own = own + recv_near[h, side].astype(F32)
        sums[pl.ds(h * half_slots, half_slots)] = own.reshape(half_slots, 8, width).astype(BF16)
        if h == 0:
            pltpu.make_async_copy(sums.at[my_member], ret.at[my_member], r_recv.at[0]).start()
        for c in range(4 * h, 4 * h + 4):
            for r in range(MEMBERS):
                if c == 0 and r == 0:
                    continue
                member = (my_member + r) % MEMBERS
                r_copy(c, member, device(-OFFSETS[c], member)).start()

    for step in range(PLANES + 2):
        if step < PLANES:
            gather_first(step)
        if 0 <= step - 1 < PLANES:
            gather_relay(step - 1)
        if 0 <= step - 2 < PLANES:
            gather_last(step - 2)
    for copy in weight_copies:
        copy.wait()
    for h in range(2):
        unpack_chunks(4 * h, 4)
        forward(h)
        scatter_far(h)
        scatter_near(h)
        scatter_own(h)

    for h in range(2):
        at = pl.ds(h * half_slots, half_slots)
        pltpu.make_async_copy(sums.at[at], ret.at[at], r_recv.at[h]).wait()
    back = ret[...].astype(F32).reshape(experts * 8, width).astype(BF16)
    out_ref[...] = lax.dot_general(select[...], back, TN, preferred_element_type=F32).astype(BF16)

    for c in range(PLANES):
        count = MEMBERS - 1 if c == 0 else MEMBERS
        at = pl.ds(c * MEMBERS, count)
        pltpu.make_async_copy(pack.at[at], xin.at[0, at], a_send.at[c]).wait()
    for c in range(PLANES):
        for side in range(2):
            y_copy(side, c).wait_send()
            o_copy(side, c).wait_send()
    for h in range(2):
        for side in range(2):
            far_copy(side, h).wait_send()
            near_copy(side, h).wait_send()
        count = half_slots - 1 if h == 0 else half_slots
        at = pl.ds(h * half_slots, count)
        pltpu.make_async_copy(sums.at[at], ret.at[at], r_send.at[h]).wait()


def per_device(tokens, out_grads, species, expert_table, gate_weight, up_weight, down_weight):
    experts = expert_table.shape[0]
    tensor_size = lax.axis_size("tensor")
    count, width = tokens.shape
    capacity = 2 * (count // tensor_size) // experts
    depth, hidden = gate_weight.shape[1:]
    all_rows = experts * tensor_size * capacity
    vmem = pl.BlockSpec(memory_space=pltpu.VMEM)
    hbm = pl.BlockSpec(memory_space=pl.ANY)
    dma = pltpu.SemaphoreType.DMA
    return pl.pallas_call(
        functools.partial(kernel, capacity),
        out_shape=jax.ShapeDtypeStruct((count, width), BF16),
        in_specs=[vmem, vmem, vmem, pl.BlockSpec(memory_space=pltpu.SMEM), hbm, hbm, hbm],
        out_specs=vmem,
        scratch_shapes=[
            pltpu.VMEM((experts, 16, width), BF16),
            pltpu.VMEM((tensor_size, experts, 16, width), BF16),
            pltpu.VMEM((all_rows, depth), BF16),
            pltpu.VMEM((all_rows, depth), BF16),
            pltpu.VMEM((depth, hidden), BF16),
            pltpu.VMEM((depth, hidden), BF16),
            pltpu.VMEM((hidden, depth), BF16),
            pltpu.VMEM((2, all_rows // 2, hidden), BF16),
            pltpu.VMEM((2, all_rows // 2, hidden), BF16),
            pltpu.VMEM((2, 2, all_rows // 4, width), BF16),
            pltpu.VMEM((2, 2, all_rows // 2, width), BF16),
            pltpu.VMEM((2, 2, all_rows // 4, width), BF16),
            pltpu.VMEM((2, 2, all_rows // 2, width), BF16),
            pltpu.VMEM((experts, 8, width), BF16),
            pltpu.VMEM((experts, 8, width), BF16),
            pltpu.VMEM((all_rows, count), BF16),
            dma((3, 4)), dma((8,)), dma((8,)), dma((2, 8)), dma((2, 8)), dma((2, 8)), dma((2, 8)),
            dma((2, 2)), dma((2, 2)), dma((2, 2)), dma((2, 2)), dma((2,)), dma((2,)),
        ],
        compiler_params=pltpu.CompilerParams(
            collective_id=0, has_side_effects=True, vmem_limit_bytes=56 * 1024 * 1024
        ),
    )(tokens, out_grads, species.reshape(1, count), expert_table, gate_weight[0], up_weight[0], down_weight[0])


def solution(mesh):
    placed = (
        P("expert", "tensor"),
        P("expert", "tensor"),
        P("expert", None),
        P(),
        P("expert", None, "tensor"),
        P("expert", None, "tensor"),
        P("expert", "tensor", None),
    )
    return jax.shard_map(
        per_device, mesh=mesh, in_specs=placed, out_specs=P("expert", "tensor"), check_vma=False
    )
```

```python
import functools

import jax
import jax.numpy as jnp
from jax import lax
from jax.experimental import pallas as pl
from jax.experimental.pallas import tpu as pltpu
from jax.sharding import PartitionSpec as P

MESH = pl.DeviceIdType.MESH
F32 = jnp.float32
BF16 = jnp.bfloat16
NT = (((1,), (1,)), ((), ()))
PLANES, ACROSS, CORES = 8, 4, 2
CHIPS = (
    (0, 0),
    (0, 1), (0, -1), (1, 0),
    (-1, 0), (1, 1), (-1, -1), (1, -1),
    (3, 0), (-3, 0), (4, 0), (-1, 1),
    (3, 1), (-3, -1), (4, 1), (0, 2),
    (3, -1), (-3, 1), (4, -1), (2, 2),
    (3, 2), (-3, 2), (4, 2), (-2, 2),
    (2, 0), (-2, 0), (1, 2), (-1, 2),
    (2, 1), (-2, -1), (2, -1), (-2, 1),
)
UNITS = ((0, 2), (2, 6), (8, 8), (16, 8), (24, 8), (32, 8), (40, 8), (48, 8), (56, 8))
GROUPS = ((0, 32), (32, 16), (48, 16))
ROWS = 8
TILE = 512


def place_of(species, table_ref, my_plane, my_across, experts, capacity, block):
    count = species.shape[1]
    expert_of = jnp.zeros_like(species)
    for kind in range(experts):
        expert_of = jnp.where(species == kind, table_ref[kind], expert_of)
    ids = lax.broadcasted_iota(jnp.int32, (experts, count), 0)
    hits = jnp.where(ids == expert_of, 1.0, 0.0)
    before = lax.broadcasted_iota(jnp.int32, (count, count), 0)
    after = lax.broadcasted_iota(jnp.int32, (count, count), 1)
    same_block = (before // block) == (after // block)
    earlier_of = jnp.where((before < after) & same_block, 1.0, 0.0).astype(BF16)
    earlier = jnp.dot(hits.astype(BF16), earlier_of, preferred_element_type=F32)
    slot = jnp.sum(hits * earlier, axis=0, keepdims=True).astype(jnp.int32)
    away = (expert_of // (ACROSS * CORES) - my_plane + PLANES) % PLANES
    aside = ((expert_of // CORES) % ACROSS - my_across + ACROSS) % ACROSS
    step = away * ACROSS + aside
    chip = jnp.zeros_like(step)
    for k in range(1, len(CHIPS)):
        chip = jnp.where(step == (CHIPS[k][0] % PLANES) * ACROSS + CHIPS[k][1] % ACROSS, k, chip)
    block_id = lax.broadcasted_iota(jnp.int32, (1, count), 1) // block
    return (chip * CORES + expert_of % CORES) * ROWS + block_id * capacity + slot


def kernel(
    capacity,
    tokens_hbm, grads_hbm, species_hbm, table_ref, gate_hbm, up_hbm, down_hbm,
    ret, place_hbm,
    tokens_ref, grads_ref, species_ref, place_ref,
    pack, xin, rows, rgrads, early, gate_w, up_w, down_w, gate_g, up_g,
    send_far, send_near, recv_far, recv_near, sums,
    i_sem, p_sem, w_sem, a_send, a_recv, y_send, y_recv, o_send, o_recv, f_send, f_recv, n_send, n_recv, r_send, r_recv,
):
    experts = lax.axis_size("expert")
    tensor_size = lax.axis_size("tensor")
    me = lax.axis_index("expert")
    mine = lax.axis_index("tensor")
    my_plane = me // (ACROSS * CORES)
    my_across = (me // CORES) % ACROSS
    my_core = me % CORES
    right = (mine + 1) % tensor_size
    left = (mine + tensor_size - 1) % tensor_size
    width = tokens_ref.shape[1]

    def device(k, core, way=1):
        plane = (my_plane + way * CHIPS[k][0] + PLANES) % PLANES
        across = (my_across + way * CHIPS[k][1] + ACROSS) % ACROSS
        return ((plane * ACROSS + across) * CORES + core, mine)

    def cores(k):
        return (1 - my_core,) if k == 0 else (my_core, 1 - my_core)

    barrier = pltpu.get_barrier_semaphore()
    for k in reversed(range(len(CHIPS))):
        for core in cores(k):
            pl.semaphore_signal(barrier, inc=1, device_id=device(k, core), device_id_type=MESH)
    for side in (left, right):
        pl.semaphore_signal(barrier, inc=1, device_id=(me, side), device_id_type=MESH)

    inputs = [
        pltpu.make_async_copy(src, dst, i_sem.at[i])
        for i, (src, dst) in enumerate(((species_hbm, species_ref), (tokens_hbm, tokens_ref), (grads_hbm, grads_ref)))
    ]
    for copy in inputs:
        copy.start()
    inputs[0].wait()
    block = tokens_ref.shape[0] // tensor_size
    place = place_of(species_ref[...], table_ref, my_plane, my_across, experts, capacity, block)
    place_ref[...] = place
    place_out = pltpu.make_async_copy(place_ref, place_hbm, p_sem)
    place_out.start()
    inputs[1].wait()
    inputs[2].wait()

    for c in range(experts // 8):
        ids = lax.broadcasted_iota(jnp.int32, (8 * ROWS, place.shape[1]), 0) + c * 8 * ROWS
        part = jnp.where(ids == place, 1.0, 0.0).astype(BF16)
        own_rows = jnp.dot(part, tokens_ref[...], preferred_element_type=F32)
        own_grads = jnp.dot(part, grads_ref[...], preferred_element_type=F32)
        both = jnp.concatenate(
            [own_rows.reshape(8, ROWS, width), own_grads.reshape(8, ROWS, width)], axis=1
        )
        pack[pl.ds(c * 8, 8)] = both.astype(BF16)
    pl.semaphore_wait(barrier, experts - 1 + 2)

    def a_start(u):
        first, count = UNITS[u]
        for k in range(first // CORES, (first + count) // CORES):
            for core in cores(k):
                pltpu.make_async_remote_copy(
                    src_ref=pack.at[k * CORES + core],
                    dst_ref=xin.at[0, k * CORES + my_core],
                    send_sem=a_send.at[u],
                    recv_sem=a_recv.at[u],
                    device_id=device(k, core),
                    device_id_type=MESH,
                ).start()

    def span(u):
        return pl.ds(*UNITS[u])

    def y_copy(side, u):
        return pltpu.make_async_remote_copy(
            src_ref=xin.at[0, span(u)],
            dst_ref=xin.at[1 + side, span(u)],
            send_sem=y_send.at[side, u],
            recv_sem=y_recv.at[side, u],
            device_id=(me, (right, left)[side]),
            device_id_type=MESH,
        )

    def o_copy(side, u):
        first, count = UNITS[u]
        part = pl.ds(first + side * (count // 2), count // 2)
        return pltpu.make_async_remote_copy(
            src_ref=xin.at[1 + side, part],
            dst_ref=xin.at[3, part],
            send_sem=o_send.at[side, u],
            recv_sem=o_recv.at[side, u],
            device_id=(me, (right, left)[side]),
            device_id_type=MESH,
        )

    def gather_first(u):
        pltpu.make_async_copy(pack.at[span(u)], xin.at[0, span(u)], a_recv.at[u]).wait()
        for side in range(2):
            y_copy(side, u).start()

    def gather_relay(u):
        for side in range(2):
            y_copy(side, u).wait_recv()
            o_copy(side, u).start()

    def gather_last(u):
        for side in range(2):
            o_copy(side, u).wait_recv()

    def rows_of(g):
        first, count = GROUPS[g]
        return pl.ds(first * ROWS, count * ROWS)

    def split_rows(g, features):
        first, count = GROUPS[g]
        for j in features:
            both = xin[j, pl.ds(first, count)].astype(F32)
            cols = pl.ds(j * width, width)
            rows[rows_of(g), cols] = both[:, 0:ROWS, :].reshape(count * ROWS, width).astype(BF16)
            rgrads[rows_of(g), cols] = both[:, ROWS:2 * ROWS, :].reshape(count * ROWS, width).astype(BF16)

    def products(g, n, first, count):
        at = rows_of(g)
        cols = pl.ds(n * TILE, TILE)
        depth = pl.ds(first * width, count * width)
        x = rows[at, depth]
        gate = jnp.dot(x, gate_w[depth, cols], preferred_element_type=F32)
        up = jnp.dot(x, up_w[depth, cols], preferred_element_type=F32)
        hidden = lax.dot_general(rgrads[at, depth], down_w[cols, depth], NT, preferred_element_type=F32)
        return gate, up, hidden

    def finish(g, n, gate, up, hidden):
        at = rows_of(g)
        cols = pl.ds(n * TILE, TILE)
        s = jax.nn.sigmoid(gate)
        hs = hidden * s
        up_g[at, cols] = (hs * gate).astype(BF16)
        gate_g[at, cols] = (hs * up * (1.0 + gate * (1.0 - s))).astype(BF16)

    def forward(g, n):
        finish(g, n, *products(g, n, 0, 4))

    def forward_part(n):
        for i, value in enumerate(products(len(GROUPS) - 1, n, 0, 3)):
            early[i, :, pl.ds(n * TILE, TILE)] = value

    def forward_end(n):
        g = len(GROUPS) - 1
        late = products(g, n, 3, 1)
        finish(g, n, *(early[i, :, pl.ds(n * TILE, TILE)] + late[i] for i in range(3)))

    def partial(g, j):
        feats = pl.ds(j * width, width)
        at = rows_of(g)
        return lax.dot_general(gate_g[at, :], gate_w[feats, :], NT, preferred_element_type=F32) + lax.dot_general(
            up_g[at, :], up_w[feats, :], NT, preferred_element_type=F32
        )

    def half_of(g):
        first, count = GROUPS[g]
        return pl.ds(first * ROWS // 2, count * ROWS // 2)

    def far_copy(side, g):
        return pltpu.make_async_remote_copy(
            src_ref=send_far.at[side, half_of(g)],
            dst_ref=recv_far.at[side, half_of(g)],
            send_sem=f_send.at[side, g],
            recv_sem=f_recv.at[side, g],
            device_id=(me, (right, left)[side]),
            device_id_type=MESH,
        )

    def near_copy(side, g):
        return pltpu.make_async_remote_copy(
            src_ref=send_near.at[side, rows_of(g)],
            dst_ref=recv_near.at[side, rows_of(g)],
            send_sem=n_send.at[side, g],
            recv_sem=n_recv.at[side, g],
            device_id=(me, (right, left)[side]),
            device_id_type=MESH,
        )

    def scatter_far(g):
        half = GROUPS[g][1] * ROWS // 2
        far = partial(g, 3).astype(BF16)
        for side in range(2):
            send_far[side, half_of(g)] = far[side * half:(side + 1) * half]
            far_copy(side, g).start()

    def scatter_near(g):
        first = GROUPS[g][0] * ROWS
        half = GROUPS[g][1] * ROWS // 2
        for side in range(2):
            near = partial(g, 2 - side)
            far_copy(side, g).wait_recv()
            parts = [near[:half], near[half:]]
            parts[side] = parts[side] + recv_far[side, half_of(g)].astype(F32)
            for i in range(2):
                send_near[side, pl.ds(first + i * half, half)] = parts[i].astype(BF16)
            near_copy(side, g).start()

    def scatter_own(g):
        first, count = GROUPS[g]
        own = partial(g, 0)
        for side in range(2):
            near_copy(side, g).wait_recv()
            own = own + recv_near[side, rows_of(g)].astype(F32)
        sums[pl.ds(first, count)] = own.reshape(count, ROWS, width).astype(BF16)
        if g == 0:
            pltpu.make_async_copy(sums.at[my_core], ret.at[my_core], r_recv.at[0]).start()
        for k in range(first // CORES, (first + count) // CORES):
            for core in cores(k):
                pltpu.make_async_remote_copy(
                    src_ref=sums.at[k * CORES + core],
                    dst_ref=ret.at[k * CORES + my_core],
                    send_sem=r_send.at[g],
                    recv_sem=r_recv.at[g],
                    device_id=device(k, core, -1),
                    device_id_type=MESH,
                ).start()

    pltpu.make_async_copy(pack.at[my_core], xin.at[0, my_core], a_recv.at[0]).start()
    for u in range(3):
        a_start(u)
    gather_first(0)
    a_start(3)
    a_start(4)
    gather_first(1)
    for u in range(5, len(UNITS)):
        a_start(u)

    feature = (mine, left, right, (mine + 2) % tensor_size)
    weight_copies = []
    for j in range(4):
        start = pl.multiple_of(feature[j] * width, width)
        for w, (src, dst) in enumerate((
            (gate_hbm.at[pl.ds(start, width), :], gate_w.at[pl.ds(j * width, width), :]),
            (up_hbm.at[pl.ds(start, width), :], up_w.at[pl.ds(j * width, width), :]),
            (down_hbm.at[:, pl.ds(start, width)], down_w.at[:, pl.ds(j * width, width)]),
        )):
            copy = pltpu.make_async_copy(src, dst, w_sem.at[w, j])
            copy.start()
            weight_copies.append(copy)

    def weights_here():
        for copy in weight_copies:
            copy.wait()

    after = {
        3: (weights_here,),
        5: (lambda: split_rows(0, range(4)), lambda: forward(0, 0)),
        6: (lambda: forward(0, 1), lambda: scatter_far(0)),
        7: (
            lambda: scatter_near(0), lambda: split_rows(1, range(4)), lambda: forward(1, 0), lambda: forward(1, 1),
            lambda: scatter_far(1),
        ),
        8: (
            lambda: split_rows(2, range(3)), lambda: forward_part(0), lambda: forward_part(1),
            lambda: scatter_near(1),
        ),
    }
    for u in range(len(UNITS)):
        if u >= 1 and u + 1 < len(UNITS):
            gather_first(u + 1)
        gather_relay(u)
        if u >= 1:
            gather_last(u - 1)
        for task in after.get(u, ()):
            task()
    gather_last(len(UNITS) - 1)
    split_rows(2, (3,))
    forward_end(0)
    forward_end(1)
    scatter_far(2)
    scatter_own(0)
    scatter_near(2)
    scatter_own(1)
    scatter_own(2)

    place_out.wait()
    for u in range(len(UNITS)):
        first, count = UNITS[u]
        at = pl.ds(first, count - 1 if u == 0 else count)
        pltpu.make_async_copy(pack.at[at], xin.at[0, at], a_send.at[u]).wait()
        for side in range(2):
            y_copy(side, u).wait_send()
            o_copy(side, u).wait_send()
    for g in range(len(GROUPS)):
        for side in range(2):
            far_copy(side, g).wait_send()
            near_copy(side, g).wait_send()
        first, count = GROUPS[g]
        at = pl.ds(first, count - 1 if g == 0 else count)
        pltpu.make_async_copy(sums.at[at], ret.at[at], r_send.at[g]).wait()
    for g in range(len(GROUPS)):
        at = pl.ds(*GROUPS[g])
        pltpu.make_async_copy(sums.at[at], ret.at[at], r_recv.at[g]).wait()


def per_device(tokens, out_grads, species, expert_table, gate_weight, up_weight, down_weight):
    experts = expert_table.shape[0]
    tensor_size = lax.axis_size("tensor")
    count, width = tokens.shape
    capacity = 2 * (count // tensor_size) // experts
    depth, hidden = gate_weight.shape[1:]
    all_rows = experts * ROWS
    hbm = pl.BlockSpec(memory_space=pl.ANY)
    dma = pltpu.SemaphoreType.DMA
    units, groups = len(UNITS), len(GROUPS)
    returned, place = pl.pallas_call(
        functools.partial(kernel, capacity),
        out_shape=(
            pltpu.VMEM((experts, ROWS, width), BF16),
            jax.ShapeDtypeStruct((1, count), jnp.int32),
        ),
        in_specs=[hbm, hbm, hbm, pl.BlockSpec(memory_space=pltpu.SMEM), hbm, hbm, hbm],
        out_specs=(pl.BlockSpec(memory_space=pltpu.VMEM), hbm),
        scratch_shapes=[
            pltpu.VMEM((count, width), BF16),
            pltpu.VMEM((count, width), BF16),
            pltpu.VMEM((1, count), jnp.int32),
            pltpu.VMEM((1, count), jnp.int32),
            pltpu.VMEM((experts, 2 * ROWS, width), BF16),
            pltpu.VMEM((tensor_size, experts, 2 * ROWS, width), BF16),
            pltpu.VMEM((all_rows, depth), BF16),
            pltpu.VMEM((all_rows, depth), BF16),
            pltpu.VMEM((3, GROUPS[-1][1] * ROWS, hidden), F32),
            pltpu.VMEM((depth, hidden), BF16),
            pltpu.VMEM((depth, hidden), BF16),
            pltpu.VMEM((hidden, depth), BF16),
            pltpu.VMEM((all_rows, hidden), BF16),
            pltpu.VMEM((all_rows, hidden), BF16),
            pltpu.VMEM((2, all_rows // 2, width), BF16),
            pltpu.VMEM((2, all_rows, width), BF16),
            pltpu.VMEM((2, all_rows // 2, width), BF16),
            pltpu.VMEM((2, all_rows, width), BF16),
            pltpu.VMEM((experts, ROWS, width), BF16),
            dma((3,)), dma, dma((3, 4)), dma((units,)), dma((units,)),
            dma((2, units)), dma((2, units)), dma((2, units)), dma((2, units)),
            dma((2, groups)), dma((2, groups)), dma((2, groups)), dma((2, groups)), dma((groups,)), dma((groups,)),
        ],
        compiler_params=pltpu.CompilerParams(
            collective_id=0, has_side_effects=True, vmem_limit_bytes=56 * 1024 * 1024
        ),
    )(tokens, out_grads, species.reshape(1, count), expert_table, gate_weight[0], up_weight[0], down_weight[0])
    ids = lax.broadcasted_iota(jnp.int32, (count, all_rows), 1)
    chosen = (ids == place.reshape(count, 1)).astype(BF16)
    return jnp.dot(chosen, returned.reshape(all_rows, width), preferred_element_type=F32).astype(BF16)


def solution(mesh):
    placed = (
        P("expert", "tensor"),
        P("expert", "tensor"),
        P("expert", None),
        P(),
        P("expert", None, "tensor"),
        P("expert", None, "tensor"),
        P("expert", "tensor", None),
    )
    return jax.shard_map(
        per_device, mesh=mesh, in_specs=placed, out_specs=P("expert", "tensor"), check_vma=False
    )
```

```python
import functools

import jax
import jax.numpy as jnp
from jax import lax
from jax.experimental import pallas as pl
from jax.experimental.pallas import tpu as pltpu
from jax.sharding import PartitionSpec as P

MESH = pl.DeviceIdType.MESH
F32 = jnp.float32
BF16 = jnp.bfloat16
NT = (((1,), (1,)), ((), ()))
PLANES, ACROSS, CORES = 8, 4, 2
CHIPS = (
    (0, 0),
    (0, 1), (0, -1), (1, 0),
    (-1, 0), (1, 1), (-1, -1), (1, -1),
    (3, 0), (-3, 0), (4, 0), (-1, 1),
    (3, 1), (-3, -1), (4, 1), (0, 2),
    (3, -1), (-3, 1), (4, -1), (2, 2),
    (3, 2), (-3, 2), (4, 2), (-2, 2),
    (2, 0), (-2, 0), (1, 2), (-1, 2),
    (2, 1), (-2, -1), (2, -1), (-2, 1),
)
UNITS = ((0, 2), (2, 6), (8, 8), (16, 8), (24, 8), (32, 8), (40, 8), (48, 8), (56, 8))
GROUPS = ((0, 32), (32, 16), (48, 16))
ROWS = 8
TILE = 512


def place_of(species, table_ref, my_plane, my_across, experts, capacity, block):
    count = species.shape[1]
    expert_of = jnp.zeros_like(species)
    for kind in range(experts):
        expert_of = jnp.where(species == kind, table_ref[kind], expert_of)
    ids = lax.broadcasted_iota(jnp.int32, (experts, count), 0)
    hits = jnp.where(ids == expert_of, 1.0, 0.0)
    before = lax.broadcasted_iota(jnp.int32, (count, count), 0)
    after = lax.broadcasted_iota(jnp.int32, (count, count), 1)
    same_block = (before // block) == (after // block)
    earlier_of = jnp.where((before < after) & same_block, 1.0, 0.0).astype(BF16)
    earlier = jnp.dot(hits.astype(BF16), earlier_of, preferred_element_type=F32)
    slot = jnp.sum(hits * earlier, axis=0, keepdims=True).astype(jnp.int32)
    away = (expert_of // (ACROSS * CORES) - my_plane + PLANES) % PLANES
    aside = ((expert_of // CORES) % ACROSS - my_across + ACROSS) % ACROSS
    step = away * ACROSS + aside
    chip = jnp.zeros_like(step)
    for k in range(1, len(CHIPS)):
        chip = jnp.where(step == (CHIPS[k][0] % PLANES) * ACROSS + CHIPS[k][1] % ACROSS, k, chip)
    block_id = lax.broadcasted_iota(jnp.int32, (1, count), 1) // block
    return (chip * CORES + expert_of % CORES) * ROWS + block_id * capacity + slot


def kernel(
    capacity,
    tokens_hbm, grads_hbm, species_hbm, table_hbm, gate_hbm, up_hbm, down_hbm,
    ret, place_hbm,
    tokens_ref, grads_ref, species_ref, table_ref, place_ref,
    pack, xin, rows, rgrads, early, gate_w, up_w, down_w, gate_g, up_g,
    send_far, send_near, recv_far, recv_near, sums,
    i_sem, p_sem, w_sem, a_send, a_recv, y_send, y_recv, o_send, o_recv, f_send, f_recv, n_send, n_recv, r_send, r_recv,
):
    experts = lax.axis_size("expert")
    tensor_size = lax.axis_size("tensor")
    me = lax.axis_index("expert")
    mine = lax.axis_index("tensor")
    my_plane = me // (ACROSS * CORES)
    my_across = (me // CORES) % ACROSS
    my_core = me % CORES
    right = (mine + 1) % tensor_size
    left = (mine + tensor_size - 1) % tensor_size
    width = tokens_ref.shape[1]

    def device(k, core, way=1):
        plane = (my_plane + way * CHIPS[k][0] + PLANES) % PLANES
        across = (my_across + way * CHIPS[k][1] + ACROSS) % ACROSS
        return ((plane * ACROSS + across) * CORES + core, mine)

    def cores(k):
        return (1 - my_core,) if k == 0 else (my_core, 1 - my_core)

    barrier = pltpu.get_barrier_semaphore()
    for k in reversed(range(len(CHIPS))):
        for core in cores(k):
            pl.semaphore_signal(barrier, inc=1, device_id=device(k, core), device_id_type=MESH)
    for side in (left, right):
        pl.semaphore_signal(barrier, inc=1, device_id=(me, side), device_id_type=MESH)

    inputs = [
        pltpu.make_async_copy(src, dst, i_sem.at[i])
        for i, (src, dst) in enumerate(((species_hbm, species_ref), (table_hbm, table_ref), (tokens_hbm, tokens_ref), (grads_hbm, grads_ref)))
    ]
    for copy in inputs:
        copy.start()
    inputs[0].wait()
    inputs[1].wait()
    block = tokens_ref.shape[0] // tensor_size
    place = place_of(species_ref[...], table_ref, my_plane, my_across, experts, capacity, block)
    place_ref[...] = place
    place_out = pltpu.make_async_copy(place_ref, place_hbm, p_sem)
    place_out.start()
    inputs[2].wait()
    inputs[3].wait()

    for c in range(experts // 8):
        ids = lax.broadcasted_iota(jnp.int32, (8 * ROWS, place.shape[1]), 0) + c * 8 * ROWS
        part = jnp.where(ids == place, 1.0, 0.0).astype(BF16)
        own_rows = jnp.dot(part, tokens_ref[...], preferred_element_type=F32)
        own_grads = jnp.dot(part, grads_ref[...], preferred_element_type=F32)
        both = jnp.concatenate(
            [own_rows.reshape(8, ROWS, width), own_grads.reshape(8, ROWS, width)], axis=1
        )
        pack[pl.ds(c * 8, 8)] = both.astype(BF16)
    pl.semaphore_wait(barrier, experts - 1 + 2)

    def a_start(u):
        first, count = UNITS[u]
        for k in range(first // CORES, (first + count) // CORES):
            for core in cores(k):
                pltpu.make_async_remote_copy(
                    src_ref=pack.at[k * CORES + core],
                    dst_ref=xin.at[0, k * CORES + my_core],
                    send_sem=a_send,
                    recv_sem=a_recv.at[u],
                    device_id=device(k, core),
                    device_id_type=MESH,
                ).start()

    def span(u):
        return pl.ds(*UNITS[u])

    def y_copy(side, u):
        return pltpu.make_async_remote_copy(
            src_ref=xin.at[0, span(u)],
            dst_ref=xin.at[1 + side, span(u)],
            send_sem=y_send.at[side],
            recv_sem=y_recv.at[side, u],
            device_id=(me, (right, left)[side]),
            device_id_type=MESH,
        )

    def o_copy(side, u):
        first, count = UNITS[u]
        part = pl.ds(first + side * (count // 2), count // 2)
        return pltpu.make_async_remote_copy(
            src_ref=xin.at[1 + side, part],
            dst_ref=xin.at[3, part],
            send_sem=o_send.at[side],
            recv_sem=o_recv.at[side, u],
            device_id=(me, (right, left)[side]),
            device_id_type=MESH,
        )

    def gather_first(u):
        pltpu.make_async_copy(pack.at[span(u)], xin.at[0, span(u)], a_recv.at[u]).wait()
        for side in range(2):
            y_copy(side, u).start()

    def gather_relay(u):
        for side in range(2):
            y_copy(side, u).wait_recv()
            o_copy(side, u).start()

    def gather_last(u):
        for side in range(2):
            o_copy(side, u).wait_recv()

    def arrived(first, end):
        for u in range(first, end):
            gather_last(u)

    def rows_of(g):
        first, count = GROUPS[g]
        return pl.ds(first * ROWS, count * ROWS)

    def split_rows(g, features):
        first, count = GROUPS[g]
        for j in features:
            both = xin[j, pl.ds(first, count)].astype(F32)
            cols = pl.ds(j * width, width)
            rows[rows_of(g), cols] = both[:, 0:ROWS, :].reshape(count * ROWS, width).astype(BF16)
            rgrads[rows_of(g), cols] = both[:, ROWS:2 * ROWS, :].reshape(count * ROWS, width).astype(BF16)

    def products(g, n, first, count):
        at = rows_of(g)
        cols = pl.ds(n * TILE, TILE)
        depth = pl.ds(first * width, count * width)
        x = rows[at, depth]
        gate = jnp.dot(x, gate_w[depth, cols], preferred_element_type=F32)
        up = jnp.dot(x, up_w[depth, cols], preferred_element_type=F32)
        hidden = lax.dot_general(rgrads[at, depth], down_w[cols, depth], NT, preferred_element_type=F32)
        return gate, up, hidden

    def finish(g, n, gate, up, hidden):
        at = rows_of(g)
        cols = pl.ds(n * TILE, TILE)
        s = jax.nn.sigmoid(gate)
        hs = hidden * s
        up_g[at, cols] = (hs * gate).astype(BF16)
        gate_g[at, cols] = (hs * up * (1.0 + gate * (1.0 - s))).astype(BF16)

    def forward(g, n):
        finish(g, n, *products(g, n, 0, 4))

    def forward_part(n):
        for i, value in enumerate(products(len(GROUPS) - 1, n, 0, 3)):
            early[i, :, pl.ds(n * TILE, TILE)] = value

    def forward_end(n):
        g = len(GROUPS) - 1
        late = products(g, n, 3, 1)
        finish(g, n, *(early[i, :, pl.ds(n * TILE, TILE)] + late[i] for i in range(3)))

    def partial(g, j):
        feats = pl.ds(j * width, width)
        at = rows_of(g)
        return lax.dot_general(gate_g[at, :], gate_w[feats, :], NT, preferred_element_type=F32) + lax.dot_general(
            up_g[at, :], up_w[feats, :], NT, preferred_element_type=F32
        )

    def half_of(g):
        first, count = GROUPS[g]
        return pl.ds(first * ROWS // 2, count * ROWS // 2)

    def far_copy(side, g):
        return pltpu.make_async_remote_copy(
            src_ref=send_far.at[side, half_of(g)],
            dst_ref=recv_far.at[side, half_of(g)],
            send_sem=f_send.at[side],
            recv_sem=f_recv.at[side, g],
            device_id=(me, (right, left)[side]),
            device_id_type=MESH,
        )

    def near_copy(side, g):
        return pltpu.make_async_remote_copy(
            src_ref=send_near.at[side, rows_of(g)],
            dst_ref=recv_near.at[side, rows_of(g)],
            send_sem=n_send.at[side],
            recv_sem=n_recv.at[side, g],
            device_id=(me, (right, left)[side]),
            device_id_type=MESH,
        )

    def scatter_far(g):
        half = GROUPS[g][1] * ROWS // 2
        far = partial(g, 3).astype(BF16)
        for side in range(2):
            send_far[side, half_of(g)] = far[side * half:(side + 1) * half]
            far_copy(side, g).start()

    def scatter_near(g):
        first = GROUPS[g][0] * ROWS
        half = GROUPS[g][1] * ROWS // 2
        for side in range(2):
            near = partial(g, 2 - side)
            far_copy(side, g).wait_recv()
            parts = [near[:half], near[half:]]
            parts[side] = parts[side] + recv_far[side, half_of(g)].astype(F32)
            for i in range(2):
                send_near[side, pl.ds(first + i * half, half)] = parts[i].astype(BF16)
            near_copy(side, g).start()

    def scatter_own(g):
        first, count = GROUPS[g]
        own = partial(g, 0)
        for side in range(2):
            near_copy(side, g).wait_recv()
            own = own + recv_near[side, rows_of(g)].astype(F32)
        sums[pl.ds(first, count)] = own.reshape(count, ROWS, width).astype(BF16)
        if g == 0:
            pltpu.make_async_copy(sums.at[my_core], ret.at[my_core], r_recv.at[0]).start()
        for k in range(first // CORES, (first + count) // CORES):
            for core in cores(k):
                pltpu.make_async_remote_copy(
                    src_ref=sums.at[k * CORES + core],
                    dst_ref=ret.at[k * CORES + my_core],
                    send_sem=r_send,
                    recv_sem=r_recv.at[g],
                    device_id=device(k, core, -1),
                    device_id_type=MESH,
                ).start()

    pltpu.make_async_copy(pack.at[my_core], xin.at[0, my_core], a_recv.at[0]).start()
    for u in range(3):
        a_start(u)
    gather_first(0)
    a_start(3)
    a_start(4)
    gather_first(1)
    for u in range(5, len(UNITS)):
        a_start(u)
    gather_first(2)

    feature = (mine, left, right, (mine + 2) % tensor_size)
    for j in range(4):
        start = pl.multiple_of(feature[j] * width, width)
        own = pl.ds(j * width, width)
        pltpu.make_async_copy(gate_hbm.at[pl.ds(start, width), :], gate_w.at[own, :], w_sem.at[0]).start()
        pltpu.make_async_copy(up_hbm.at[pl.ds(start, width), :], up_w.at[own, :], w_sem.at[1]).start()
        pltpu.make_async_copy(down_hbm.at[:, pl.ds(start, width)], down_w.at[:, own], w_sem.at[2]).start()

    def weights_here():
        for i, (src, dst) in enumerate(((gate_hbm, gate_w), (up_hbm, up_w), (down_hbm, down_w))):
            pltpu.make_async_copy(src, dst, w_sem.at[i]).wait()

    after = {
        3: (weights_here,),
        5: (lambda: arrived(0, 5), lambda: split_rows(0, range(4)), lambda: forward(0, 0)),
        6: (lambda: forward(0, 1), lambda: scatter_far(0)),
        7: (
            lambda: arrived(5, 7), lambda: split_rows(1, range(4)), lambda: forward(1, 0), lambda: scatter_near(0),
        ),
        8: (
            lambda: forward(1, 1), lambda: scatter_far(1),
            lambda: split_rows(2, range(3)), lambda: forward_part(0), lambda: forward_part(1),
            lambda: scatter_own(0),
        ),
    }
    for u in range(len(UNITS)):
        if u >= 2 and u + 1 < len(UNITS):
            gather_first(u + 1)
        gather_relay(u)
        for task in after.get(u, ()):
            task()
    arrived(7, 9)
    split_rows(2, (3,))
    forward_end(0)
    forward_end(1)
    scatter_near(1)
    scatter_far(2)
    scatter_own(1)
    scatter_near(2)
    scatter_own(2)

    place_out.wait()
    others = pl.ds(0, experts - 1)
    pltpu.make_async_copy(pack.at[others], xin.at[0, others], a_send).wait()
    pltpu.make_async_copy(sums.at[others], ret.at[others], r_send).wait()
    for side in range(2):
        relayed = pl.ds(0, experts // 2)
        pltpu.make_async_copy(xin.at[0], xin.at[1 + side], y_send.at[side]).wait()
        pltpu.make_async_copy(xin.at[1 + side, relayed], xin.at[3, relayed], o_send.at[side]).wait()
        pltpu.make_async_copy(send_far.at[side], recv_far.at[side], f_send.at[side]).wait()
        pltpu.make_async_copy(send_near.at[side], recv_near.at[side], n_send.at[side]).wait()
    for g in range(len(GROUPS)):
        at = pl.ds(*GROUPS[g])
        pltpu.make_async_copy(sums.at[at], ret.at[at], r_recv.at[g]).wait()


def per_device(tokens, out_grads, species, expert_table, gate_weight, up_weight, down_weight):
    experts = expert_table.shape[0]
    tensor_size = lax.axis_size("tensor")
    count, width = tokens.shape
    capacity = 2 * (count // tensor_size) // experts
    depth, hidden = gate_weight.shape[1:]
    all_rows = experts * ROWS
    hbm = pl.BlockSpec(memory_space=pl.ANY)
    dma = pltpu.SemaphoreType.DMA
    units, groups = len(UNITS), len(GROUPS)
    returned, place = pl.pallas_call(
        functools.partial(kernel, capacity),
        out_shape=(
            pltpu.VMEM((experts, ROWS, width), BF16),
            jax.ShapeDtypeStruct((1, count), jnp.int32),
        ),
        in_specs=[hbm] * 7,
        out_specs=(pl.BlockSpec(memory_space=pltpu.VMEM), hbm),
        scratch_shapes=[
            pltpu.VMEM((count, width), BF16),
            pltpu.VMEM((count, width), BF16),
            pltpu.VMEM((1, count), jnp.int32),
            pltpu.SMEM((experts,), jnp.int32),
            pltpu.VMEM((1, count), jnp.int32),
            pltpu.VMEM((experts, 2 * ROWS, width), BF16),
            pltpu.VMEM((tensor_size, experts, 2 * ROWS, width), BF16),
            pltpu.VMEM((all_rows, depth), BF16),
            pltpu.VMEM((all_rows, depth), BF16),
            pltpu.VMEM((3, GROUPS[-1][1] * ROWS, hidden), F32),
            pltpu.VMEM((depth, hidden), BF16),
            pltpu.VMEM((depth, hidden), BF16),
            pltpu.VMEM((hidden, depth), BF16),
            pltpu.VMEM((all_rows, hidden), BF16),
            pltpu.VMEM((all_rows, hidden), BF16),
            pltpu.VMEM((2, all_rows // 2, width), BF16),
            pltpu.VMEM((2, all_rows, width), BF16),
            pltpu.VMEM((2, all_rows // 2, width), BF16),
            pltpu.VMEM((2, all_rows, width), BF16),
            pltpu.VMEM((experts, ROWS, width), BF16),
            dma((4,)), dma, dma((3,)), dma, dma((units,)),
            dma((2,)), dma((2, units)), dma((2,)), dma((2, units)),
            dma((2,)), dma((2, groups)), dma((2,)), dma((2, groups)), dma, dma((groups,)),
        ],
        compiler_params=pltpu.CompilerParams(
            collective_id=0, has_side_effects=True, vmem_limit_bytes=56 * 1024 * 1024
        ),
    )(tokens, out_grads, species.reshape(1, count), expert_table, gate_weight[0], up_weight[0], down_weight[0])
    ids = lax.broadcasted_iota(jnp.int32, (count, all_rows), 1)
    chosen = (ids == place.reshape(count, 1)).astype(BF16)
    return jnp.dot(chosen, returned.reshape(all_rows, width), preferred_element_type=F32).astype(BF16)


def solution(mesh):
    placed = (
        P("expert", "tensor"),
        P("expert", "tensor"),
        P("expert", None),
        P(),
        P("expert", None, "tensor"),
        P("expert", None, "tensor"),
        P("expert", "tensor", None),
    )
    return jax.shard_map(
        per_device, mesh=mesh, in_specs=placed, out_specs=P("expert", "tensor"), check_vma=False
    )
```

```python
import functools

import jax
import jax.numpy as jnp
from jax import lax
from jax.experimental import pallas as pl
from jax.experimental.pallas import tpu as pltpu
from jax.sharding import PartitionSpec as P

MESH = pl.DeviceIdType.MESH
F32 = jnp.float32
BF16 = jnp.bfloat16
NT = (((1,), (1,)), ((), ()))
PLANES, ACROSS, CORES = 8, 4, 2
CHIPS = (
    (0, 0),
    (0, 1), (0, -1), (1, 0),
    (-1, 0), (1, 1), (-1, -1), (1, -1),
    (3, 0), (-3, 0), (4, 0), (-1, 1),
    (3, 1), (-3, -1), (4, 1), (0, 2),
    (3, -1), (-3, 1), (4, -1), (2, 2),
    (3, 2), (-3, 2), (4, 2), (-2, 2),
    (2, 0), (-2, 0), (1, 2), (-1, 2),
    (2, 1), (-2, -1), (2, -1), (-2, 1),
)
UNITS = ((0, 2), (2, 6), (8, 8), (16, 8), (24, 8), (32, 8), (40, 8), (48, 8), (56, 8))
GROUPS = ((0, 32), (32, 16), (48, 16))
ROWS = 8
TILE = 512


def place_of(species, table_ref, my_plane, my_across, experts, capacity, block):
    count = species.shape[1]
    expert_of = jnp.zeros_like(species)
    for kind in range(experts):
        expert_of = jnp.where(species == kind, table_ref[kind], expert_of)
    ids = lax.broadcasted_iota(jnp.int32, (experts, count), 0)
    hits = jnp.where(ids == expert_of, 1.0, 0.0)
    before = lax.broadcasted_iota(jnp.int32, (count, count), 0)
    after = lax.broadcasted_iota(jnp.int32, (count, count), 1)
    same_block = (before // block) == (after // block)
    earlier_of = jnp.where((before < after) & same_block, 1.0, 0.0).astype(BF16)
    earlier = jnp.dot(hits.astype(BF16), earlier_of, preferred_element_type=F32)
    slot = jnp.sum(hits * earlier, axis=0, keepdims=True).astype(jnp.int32)
    away = (expert_of // (ACROSS * CORES) - my_plane + PLANES) % PLANES
    aside = ((expert_of // CORES) % ACROSS - my_across + ACROSS) % ACROSS
    step = away * ACROSS + aside
    chip = jnp.zeros_like(step)
    for k in range(1, len(CHIPS)):
        chip = jnp.where(step == (CHIPS[k][0] % PLANES) * ACROSS + CHIPS[k][1] % ACROSS, k, chip)
    block_id = lax.broadcasted_iota(jnp.int32, (1, count), 1) // block
    return (chip * CORES + expert_of % CORES) * ROWS + block_id * capacity + slot


def kernel(
    capacity,
    tokens_hbm, grads_hbm, species_hbm, table_hbm, gate_hbm, up_hbm, down_hbm,
    ret, place_hbm,
    tokens_ref, grads_ref, species_ref, table_ref, place_ref,
    pack, xin, rows, rgrads, early, gate_w, up_w, down_w, gate_g, up_g,
    send_far, send_near, recv_far, recv_near, sums,
    i_sem, p_sem, w_sem, a_send, a_recv, y_send, y_recv, o_send, o_recv, f_send, f_recv, n_send, n_recv, r_send, r_recv,
):
    experts = lax.axis_size("expert")
    tensor_size = lax.axis_size("tensor")
    me = lax.axis_index("expert")
    mine = lax.axis_index("tensor")
    my_plane = me // (ACROSS * CORES)
    my_across = (me // CORES) % ACROSS
    my_core = me % CORES
    right = (mine + 1) % tensor_size
    left = (mine + tensor_size - 1) % tensor_size
    width = tokens_ref.shape[1]

    def device(k, core, way=1):
        plane = (my_plane + way * CHIPS[k][0] + PLANES) % PLANES
        across = (my_across + way * CHIPS[k][1] + ACROSS) % ACROSS
        return ((plane * ACROSS + across) * CORES + core, mine)

    def cores(k):
        return (1 - my_core,) if k == 0 else (my_core, 1 - my_core)

    barrier = pltpu.get_barrier_semaphore()
    for k in reversed(range(len(CHIPS))):
        for core in cores(k):
            pl.semaphore_signal(barrier, inc=1, device_id=device(k, core), device_id_type=MESH)
    for side in (left, right):
        pl.semaphore_signal(barrier, inc=1, device_id=(me, side), device_id_type=MESH)

    inputs = [
        pltpu.make_async_copy(src, dst, i_sem.at[i])
        for i, (src, dst) in enumerate(((species_hbm, species_ref), (table_hbm, table_ref), (tokens_hbm, tokens_ref), (grads_hbm, grads_ref)))
    ]
    for copy in inputs:
        copy.start()
    inputs[0].wait()
    inputs[1].wait()
    block = tokens_ref.shape[0] // tensor_size
    place = place_of(species_ref[...], table_ref, my_plane, my_across, experts, capacity, block)
    place_ref[...] = place
    place_out = pltpu.make_async_copy(place_ref, place_hbm, p_sem)
    place_out.start()
    inputs[2].wait()
    inputs[3].wait()

    for c in range(experts // 8):
        ids = lax.broadcasted_iota(jnp.int32, (8 * ROWS, place.shape[1]), 0) + c * 8 * ROWS
        part = jnp.where(ids == place, 1.0, 0.0).astype(BF16)
        own_rows = jnp.dot(part, tokens_ref[...], preferred_element_type=F32)
        own_grads = jnp.dot(part, grads_ref[...], preferred_element_type=F32)
        both = jnp.concatenate(
            [own_rows.reshape(8, ROWS, width), own_grads.reshape(8, ROWS, width)], axis=1
        )
        pack[pl.ds(c * 8, 8)] = both.astype(BF16)
    pl.semaphore_wait(barrier, experts - 1 + 2)

    def a_start(u):
        first, count = UNITS[u]
        for k in range(first // CORES, (first + count) // CORES):
            for core in cores(k):
                pltpu.make_async_remote_copy(
                    src_ref=pack.at[k * CORES + core],
                    dst_ref=xin.at[0, k * CORES + my_core],
                    send_sem=a_send,
                    recv_sem=a_recv.at[u],
                    device_id=device(k, core),
                    device_id_type=MESH,
                ).start()

    def span(u):
        return pl.ds(*UNITS[u])

    def y_copy(side, u):
        return pltpu.make_async_remote_copy(
            src_ref=xin.at[0, span(u)],
            dst_ref=xin.at[1 + side, span(u)],
            send_sem=y_send.at[side],
            recv_sem=y_recv.at[side, u],
            device_id=(me, (right, left)[side]),
            device_id_type=MESH,
        )

    def o_copy(side, u):
        first, count = UNITS[u]
        part = pl.ds(first + side * (count // 2), count // 2)
        return pltpu.make_async_remote_copy(
            src_ref=xin.at[1 + side, part],
            dst_ref=xin.at[3, part],
            send_sem=o_send.at[side],
            recv_sem=o_recv.at[side, u],
            device_id=(me, (right, left)[side]),
            device_id_type=MESH,
        )

    def gather_first(u):
        pltpu.make_async_copy(pack.at[span(u)], xin.at[0, span(u)], a_recv.at[u]).wait()
        for side in range(2):
            y_copy(side, u).start()

    def gather_relay(u):
        for side in range(2):
            y_copy(side, u).wait_recv()
            o_copy(side, u).start()

    def gather_last(u):
        for side in range(2):
            o_copy(side, u).wait_recv()

    def arrived(first, end):
        for u in range(first, end):
            gather_last(u)

    def rows_of(g):
        first, count = GROUPS[g]
        return pl.ds(first * ROWS, count * ROWS)

    def split_rows(g, features):
        first, count = GROUPS[g]
        for j in features:
            both = xin[j, pl.ds(first, count)].astype(F32)
            cols = pl.ds(j * width, width)
            rows[rows_of(g), cols] = both[:, 0:ROWS, :].reshape(count * ROWS, width).astype(BF16)
            rgrads[rows_of(g), cols] = both[:, ROWS:2 * ROWS, :].reshape(count * ROWS, width).astype(BF16)

    def products(g, n, first, count):
        at = rows_of(g)
        cols = pl.ds(n * TILE, TILE)
        depth = pl.ds(first * width, count * width)
        x = rows[at, depth]
        gate = jnp.dot(x, gate_w[depth, cols], preferred_element_type=F32)
        up = jnp.dot(x, up_w[depth, cols], preferred_element_type=F32)
        hidden = lax.dot_general(rgrads[at, depth], down_w[cols, depth], NT, preferred_element_type=F32)
        return gate, up, hidden

    def finish(g, n, gate, up, hidden):
        at = rows_of(g)
        cols = pl.ds(n * TILE, TILE)
        s = jax.nn.sigmoid(gate)
        hs = hidden * s
        up_g[at, cols] = (hs * gate).astype(BF16)
        gate_g[at, cols] = (hs * up * (1.0 + gate * (1.0 - s))).astype(BF16)

    def forward(g, n):
        finish(g, n, *products(g, n, 0, 4))

    def forward_part(n):
        for i, value in enumerate(products(len(GROUPS) - 1, n, 0, 3)):
            early[i, :, pl.ds(n * TILE, TILE)] = value

    def forward_end(n):
        g = len(GROUPS) - 1
        late = products(g, n, 3, 1)
        finish(g, n, *(early[i, :, pl.ds(n * TILE, TILE)] + late[i] for i in range(3)))

    def partial(g, j):
        feats = pl.ds(j * width, width)
        at = rows_of(g)
        return lax.dot_general(gate_g[at, :], gate_w[feats, :], NT, preferred_element_type=F32) + lax.dot_general(
            up_g[at, :], up_w[feats, :], NT, preferred_element_type=F32
        )

    def half_of(g):
        first, count = GROUPS[g]
        return pl.ds(first * ROWS // 2, count * ROWS // 2)

    def far_copy(side, g):
        return pltpu.make_async_remote_copy(
            src_ref=send_far.at[side, half_of(g)],
            dst_ref=recv_far.at[side, half_of(g)],
            send_sem=f_send.at[side],
            recv_sem=f_recv.at[side, g],
            device_id=(me, (right, left)[side]),
            device_id_type=MESH,
        )

    def near_copy(side, g):
        return pltpu.make_async_remote_copy(
            src_ref=send_near.at[side, rows_of(g)],
            dst_ref=recv_near.at[side, rows_of(g)],
            send_sem=n_send.at[side],
            recv_sem=n_recv.at[side, g],
            device_id=(me, (right, left)[side]),
            device_id_type=MESH,
        )

    def scatter_far(g):
        half = GROUPS[g][1] * ROWS // 2
        far = partial(g, 3).astype(BF16)
        for side in range(2):
            send_far[side, half_of(g)] = far[side * half:(side + 1) * half]
            far_copy(side, g).start()

    def scatter_near(g):
        first = GROUPS[g][0] * ROWS
        half = GROUPS[g][1] * ROWS // 2
        for side in range(2):
            near = partial(g, 2 - side)
            far_copy(side, g).wait_recv()
            parts = [near[:half], near[half:]]
            parts[side] = parts[side] + recv_far[side, half_of(g)].astype(F32)
            for i in range(2):
                send_near[side, pl.ds(first + i * half, half)] = parts[i].astype(BF16)
            near_copy(side, g).start()

    def scatter_own(g):
        first, count = GROUPS[g]
        own = partial(g, 0)
        for side in range(2):
            near_copy(side, g).wait_recv()
            own = own + recv_near[side, rows_of(g)].astype(F32)
        sums[pl.ds(first, count)] = own.reshape(count, ROWS, width).astype(BF16)
        if g == 0:
            pltpu.make_async_copy(sums.at[my_core], ret.at[my_core], r_recv.at[0]).start()
        for k in range(first // CORES, (first + count) // CORES):
            for core in cores(k):
                pltpu.make_async_remote_copy(
                    src_ref=sums.at[k * CORES + core],
                    dst_ref=ret.at[k * CORES + my_core],
                    send_sem=r_send,
                    recv_sem=r_recv.at[g],
                    device_id=device(k, core, -1),
                    device_id_type=MESH,
                ).start()

    pltpu.make_async_copy(pack.at[my_core], xin.at[0, my_core], a_recv.at[0]).start()
    for u in range(3):
        a_start(u)
    gather_first(0)
    a_start(3)
    a_start(4)
    gather_first(1)
    for u in range(5, len(UNITS)):
        a_start(u)
    gather_first(2)

    feature = (mine, left, right, (mine + 2) % tensor_size)
    for j in range(4):
        start = pl.multiple_of(feature[j] * width, width)
        own = pl.ds(j * width, width)
        pltpu.make_async_copy(gate_hbm.at[pl.ds(start, width), :], gate_w.at[own, :], w_sem.at[0]).start()
        pltpu.make_async_copy(up_hbm.at[pl.ds(start, width), :], up_w.at[own, :], w_sem.at[1]).start()
        pltpu.make_async_copy(down_hbm.at[:, pl.ds(start, width)], down_w.at[:, own], w_sem.at[2]).start()

    def weights_here():
        for i, (src, dst) in enumerate(((gate_hbm, gate_w), (up_hbm, up_w), (down_hbm, down_w))):
            pltpu.make_async_copy(src, dst, w_sem.at[i]).wait()

    after = {
        3: (weights_here,),
        5: (lambda: arrived(0, 5), lambda: split_rows(0, range(4)), lambda: forward(0, 0)),
        6: (lambda: forward(0, 1), lambda: scatter_far(0)),
        7: (
            lambda: scatter_near(0), lambda: arrived(5, 7), lambda: split_rows(1, range(4)), lambda: forward(1, 0), lambda: forward(1, 1),
            lambda: scatter_far(1),
        ),
        8: (
            lambda: split_rows(2, range(3)), lambda: forward_part(0), lambda: forward_part(1),
            lambda: scatter_own(0), lambda: scatter_near(1),
        ),
    }
    for u in range(len(UNITS)):
        if u >= 2 and u + 1 < len(UNITS):
            gather_first(u + 1)
        gather_relay(u)
        for task in after.get(u, ()):
            task()
    arrived(7, 9)
    split_rows(2, (3,))
    forward_end(0)
    forward_end(1)
    scatter_far(2)
    scatter_own(1)
    scatter_near(2)
    scatter_own(2)

    place_out.wait()
    others = pl.ds(0, experts - 1)
    pltpu.make_async_copy(pack.at[others], xin.at[0, others], a_send).wait()
    pltpu.make_async_copy(sums.at[others], ret.at[others], r_send).wait()
    for side in range(2):
        relayed = pl.ds(0, experts // 2)
        pltpu.make_async_copy(xin.at[0], xin.at[1 + side], y_send.at[side]).wait()
        pltpu.make_async_copy(xin.at[1 + side, relayed], xin.at[3, relayed], o_send.at[side]).wait()
        pltpu.make_async_copy(send_far.at[side], recv_far.at[side], f_send.at[side]).wait()
        pltpu.make_async_copy(send_near.at[side], recv_near.at[side], n_send.at[side]).wait()
    for g in range(len(GROUPS)):
        at = pl.ds(*GROUPS[g])
        pltpu.make_async_copy(sums.at[at], ret.at[at], r_recv.at[g]).wait()


def per_device(tokens, out_grads, species, expert_table, gate_weight, up_weight, down_weight):
    experts = expert_table.shape[0]
    tensor_size = lax.axis_size("tensor")
    count, width = tokens.shape
    capacity = 2 * (count // tensor_size) // experts
    depth, hidden = gate_weight.shape[1:]
    all_rows = experts * ROWS
    hbm = pl.BlockSpec(memory_space=pl.ANY)
    dma = pltpu.SemaphoreType.DMA
    units, groups = len(UNITS), len(GROUPS)
    returned, place = pl.pallas_call(
        functools.partial(kernel, capacity),
        out_shape=(
            pltpu.VMEM((experts, ROWS, width), BF16),
            jax.ShapeDtypeStruct((1, count), jnp.int32),
        ),
        in_specs=[hbm] * 7,
        out_specs=(pl.BlockSpec(memory_space=pltpu.VMEM), hbm),
        scratch_shapes=[
            pltpu.VMEM((count, width), BF16),
            pltpu.VMEM((count, width), BF16),
            pltpu.VMEM((1, count), jnp.int32),
            pltpu.SMEM((experts,), jnp.int32),
            pltpu.VMEM((1, count), jnp.int32),
            pltpu.VMEM((experts, 2 * ROWS, width), BF16),
            pltpu.VMEM((tensor_size, experts, 2 * ROWS, width), BF16),
            pltpu.VMEM((all_rows, depth), BF16),
            pltpu.VMEM((all_rows, depth), BF16),
            pltpu.VMEM((3, GROUPS[-1][1] * ROWS, hidden), F32),
            pltpu.VMEM((depth, hidden), BF16),
            pltpu.VMEM((depth, hidden), BF16),
            pltpu.VMEM((hidden, depth), BF16),
            pltpu.VMEM((all_rows, hidden), BF16),
            pltpu.VMEM((all_rows, hidden), BF16),
            pltpu.VMEM((2, all_rows // 2, width), BF16),
            pltpu.VMEM((2, all_rows, width), BF16),
            pltpu.VMEM((2, all_rows // 2, width), BF16),
            pltpu.VMEM((2, all_rows, width), BF16),
            pltpu.VMEM((experts, ROWS, width), BF16),
            dma((4,)), dma, dma((3,)), dma, dma((units,)),
            dma((2,)), dma((2, units)), dma((2,)), dma((2, units)),
            dma((2,)), dma((2, groups)), dma((2,)), dma((2, groups)), dma, dma((groups,)),
        ],
        compiler_params=pltpu.CompilerParams(
            collective_id=0, has_side_effects=True, vmem_limit_bytes=56 * 1024 * 1024
        ),
    )(tokens, out_grads, species.reshape(1, count), expert_table, gate_weight[0], up_weight[0], down_weight[0])
    ids = lax.broadcasted_iota(jnp.int32, (count, all_rows), 1)
    chosen = (ids == place.reshape(count, 1)).astype(BF16)
    return jnp.dot(chosen, returned.reshape(all_rows, width), preferred_element_type=F32).astype(BF16)


def solution(mesh):
    placed = (
        P("expert", "tensor"),
        P("expert", "tensor"),
        P("expert", None),
        P(),
        P("expert", None, "tensor"),
        P("expert", None, "tensor"),
        P("expert", "tensor", None),
    )
    return jax.shard_map(
        per_device, mesh=mesh, in_specs=placed, out_specs=P("expert", "tensor"), check_vma=False
    )
```

```python
import functools

import jax
import jax.numpy as jnp
from jax import lax
from jax.experimental import pallas as pl
from jax.experimental.pallas import tpu as pltpu
from jax.sharding import PartitionSpec as P

MESH = pl.DeviceIdType.MESH
F32 = jnp.float32
BF16 = jnp.bfloat16
NT = (((1,), (1,)), ((), ()))
PLANES, ACROSS, CORES = 8, 4, 2
CHIPS = (
    (0, 0),
    (0, 1), (0, -1), (1, 0),
    (-1, 0), (1, 1), (-1, -1), (1, -1),
    (3, 0), (-3, 0), (4, 0), (-1, 1),
    (3, 1), (-3, -1), (4, 1), (0, 2),
    (3, -1), (-3, 1), (4, -1), (2, 2),
    (3, 2), (-3, 2), (4, 2), (-2, 2),
    (2, 0), (-2, 0), (1, 2), (-1, 2),
    (2, 1), (-2, -1), (2, -1), (-2, 1),
)
UNITS = ((0, 2), (2, 6), (8, 8), (16, 8), (24, 8), (32, 8), (40, 8), (48, 8), (56, 8))
GROUPS = ((0, 32), (32, 16), (48, 16))
ROWS = 8
TILE = 512


def place_of(species, table_ref, my_plane, my_across, experts, capacity, block):
    count = species.shape[1]
    expert_of = jnp.zeros_like(species)
    for kind in range(experts):
        expert_of = jnp.where(species == kind, table_ref[kind], expert_of)
    ids = lax.broadcasted_iota(jnp.int32, (experts, count), 0)
    hits = jnp.where(ids == expert_of, 1.0, 0.0)
    before = lax.broadcasted_iota(jnp.int32, (count, count), 0)
    after = lax.broadcasted_iota(jnp.int32, (count, count), 1)
    same_block = (before // block) == (after // block)
    earlier_of = jnp.where((before < after) & same_block, 1.0, 0.0).astype(BF16)
    earlier = jnp.dot(hits.astype(BF16), earlier_of, preferred_element_type=F32)
    slot = jnp.sum(hits * earlier, axis=0, keepdims=True).astype(jnp.int32)
    away = (expert_of // (ACROSS * CORES) - my_plane + PLANES) % PLANES
    aside = ((expert_of // CORES) % ACROSS - my_across + ACROSS) % ACROSS
    step = away * ACROSS + aside
    chip = jnp.zeros_like(step)
    for k in range(1, len(CHIPS)):
        chip = jnp.where(step == (CHIPS[k][0] % PLANES) * ACROSS + CHIPS[k][1] % ACROSS, k, chip)
    block_id = lax.broadcasted_iota(jnp.int32, (1, count), 1) // block
    return (chip * CORES + expert_of % CORES) * ROWS + block_id * capacity + slot


def kernel(
    capacity,
    tokens_hbm, grads_hbm, species_hbm, table_hbm, gate_hbm, up_hbm, down_hbm,
    ret, place_hbm,
    tokens_ref, grads_ref, species_ref, table_ref, place_ref,
    pack, xin, rows, rgrads, early, gate_w, up_w, down_w, gate_g, up_g,
    send_far, send_near, recv_far, recv_near, sums,
    i_sem, p_sem, w_sem, a_send, a_recv, y_send, y_recv, o_send, o_recv, f_send, f_recv, n_send, n_recv, r_send, r_recv,
):
    experts = lax.axis_size("expert")
    tensor_size = lax.axis_size("tensor")
    me = lax.axis_index("expert")
    mine = lax.axis_index("tensor")
    my_plane = me // (ACROSS * CORES)
    my_across = (me // CORES) % ACROSS
    my_core = me % CORES
    right = (mine + 1) % tensor_size
    left = (mine + tensor_size - 1) % tensor_size
    width = tokens_ref.shape[1]

    def device(k, core, way=1):
        plane = (my_plane + way * CHIPS[k][0] + PLANES) % PLANES
        across = (my_across + way * CHIPS[k][1] + ACROSS) % ACROSS
        return ((plane * ACROSS + across) * CORES + core, mine)

    def cores(k):
        return (1 - my_core,) if k == 0 else (my_core, 1 - my_core)

    barrier = pltpu.get_barrier_semaphore()
    for k in reversed(range(len(CHIPS))):
        for core in cores(k):
            pl.semaphore_signal(barrier, inc=1, device_id=device(k, core), device_id_type=MESH)
    for side in (left, right):
        pl.semaphore_signal(barrier, inc=1, device_id=(me, side), device_id_type=MESH)

    inputs = [
        pltpu.make_async_copy(src, dst, i_sem.at[i])
        for i, (src, dst) in enumerate(((species_hbm, species_ref), (table_hbm, table_ref), (tokens_hbm, tokens_ref), (grads_hbm, grads_ref)))
    ]
    for copy in inputs:
        copy.start()
    inputs[0].wait()
    inputs[1].wait()
    block = tokens_ref.shape[0] // tensor_size
    place = place_of(species_ref[...], table_ref, my_plane, my_across, experts, capacity, block)
    place_ref[...] = place
    place_out = pltpu.make_async_copy(place_ref, place_hbm, p_sem)
    place_out.start()
    inputs[2].wait()
    inputs[3].wait()

    for c in range(experts // 8):
        ids = lax.broadcasted_iota(jnp.int32, (8 * ROWS, place.shape[1]), 0) + c * 8 * ROWS
        part = jnp.where(ids == place, 1.0, 0.0).astype(BF16)
        own_rows = jnp.dot(part, tokens_ref[...], preferred_element_type=F32)
        own_grads = jnp.dot(part, grads_ref[...], preferred_element_type=F32)
        both = jnp.concatenate(
            [own_rows.reshape(8, ROWS, width), own_grads.reshape(8, ROWS, width)], axis=1
        )
        pack[pl.ds(c * 8, 8)] = both.astype(BF16)
    pl.semaphore_wait(barrier, experts - 1 + 2)

    def a_start(u):
        first, count = UNITS[u]
        for k in range(first // CORES, (first + count) // CORES):
            for core in cores(k):
                pltpu.make_async_remote_copy(
                    src_ref=pack.at[k * CORES + core],
                    dst_ref=xin.at[0, k * CORES + my_core],
                    send_sem=a_send,
                    recv_sem=a_recv.at[u],
                    device_id=device(k, core),
                    device_id_type=MESH,
                ).start()

    def span(u):
        return pl.ds(*UNITS[u])

    def y_copy(side, u):
        return pltpu.make_async_remote_copy(
            src_ref=xin.at[0, span(u)],
            dst_ref=xin.at[1 + side, span(u)],
            send_sem=y_send.at[side],
            recv_sem=y_recv.at[side, u],
            device_id=(me, (right, left)[side]),
            device_id_type=MESH,
        )

    def o_copy(side, u):
        first, count = UNITS[u]
        part = pl.ds(first + side * (count // 2), count // 2)
        return pltpu.make_async_remote_copy(
            src_ref=xin.at[1 + side, part],
            dst_ref=xin.at[3, part],
            send_sem=o_send.at[side],
            recv_sem=o_recv.at[side, u],
            device_id=(me, (right, left)[side]),
            device_id_type=MESH,
        )

    def gather_first(u):
        pltpu.make_async_copy(pack.at[span(u)], xin.at[0, span(u)], a_recv.at[u]).wait()
        for side in range(2):
            y_copy(side, u).start()

    def gather_relay(u):
        for side in range(2):
            y_copy(side, u).wait_recv()
            o_copy(side, u).start()

    def gather_last(u):
        for side in range(2):
            o_copy(side, u).wait_recv()

    def arrived(first, end):
        for u in range(first, end):
            gather_last(u)

    def rows_of(g):
        first, count = GROUPS[g]
        return pl.ds(first * ROWS, count * ROWS)

    def split_rows(g, features):
        first, count = GROUPS[g]
        for j in features:
            both = xin[j, pl.ds(first, count)].astype(F32)
            cols = pl.ds(j * width, width)
            rows[rows_of(g), cols] = both[:, 0:ROWS, :].reshape(count * ROWS, width).astype(BF16)
            rgrads[rows_of(g), cols] = both[:, ROWS:2 * ROWS, :].reshape(count * ROWS, width).astype(BF16)

    def products(g, n, first, count):
        at = rows_of(g)
        cols = pl.ds(n * TILE, TILE)
        depth = pl.ds(first * width, count * width)
        x = rows[at, depth]
        gate = jnp.dot(x, gate_w[depth, cols], preferred_element_type=F32)
        up = jnp.dot(x, up_w[depth, cols], preferred_element_type=F32)
        hidden = lax.dot_general(rgrads[at, depth], down_w[cols, depth], NT, preferred_element_type=F32)
        return gate, up, hidden

    def finish(g, n, gate, up, hidden):
        at = rows_of(g)
        cols = pl.ds(n * TILE, TILE)
        s = jax.nn.sigmoid(gate)
        hs = hidden * s
        up_g[at, cols] = (hs * gate).astype(BF16)
        gate_g[at, cols] = (hs * up * (1.0 + gate * (1.0 - s))).astype(BF16)

    def forward(g, n):
        finish(g, n, *products(g, n, 0, 4))

    def forward_part(n):
        for i, value in enumerate(products(len(GROUPS) - 1, n, 0, 3)):
            early[i, :, pl.ds(n * TILE, TILE)] = value

    def forward_end(n):
        g = len(GROUPS) - 1
        late = products(g, n, 3, 1)
        finish(g, n, *(early[i, :, pl.ds(n * TILE, TILE)] + late[i] for i in range(3)))

    def partial(g, j):
        feats = pl.ds(j * width, width)
        at = rows_of(g)
        return lax.dot_general(gate_g[at, :], gate_w[feats, :], NT, preferred_element_type=F32) + lax.dot_general(
            up_g[at, :], up_w[feats, :], NT, preferred_element_type=F32
        )

    def half_of(g):
        first, count = GROUPS[g]
        return pl.ds(first * ROWS // 2, count * ROWS // 2)

    def far_copy(side, g):
        return pltpu.make_async_remote_copy(
            src_ref=send_far.at[side, half_of(g)],
            dst_ref=recv_far.at[side, half_of(g)],
            send_sem=f_send.at[side],
            recv_sem=f_recv.at[side, g],
            device_id=(me, (right, left)[side]),
            device_id_type=MESH,
        )

    def near_copy(side, g):
        return pltpu.make_async_remote_copy(
            src_ref=send_near.at[side, rows_of(g)],
            dst_ref=recv_near.at[side, rows_of(g)],
            send_sem=n_send.at[side],
            recv_sem=n_recv.at[side, g],
            device_id=(me, (right, left)[side]),
            device_id_type=MESH,
        )

    def scatter_far(g):
        half = GROUPS[g][1] * ROWS // 2
        far = partial(g, 3).astype(BF16)
        for side in range(2):
            send_far[side, half_of(g)] = far[side * half:(side + 1) * half]
            far_copy(side, g).start()

    def scatter_near(g):
        first = GROUPS[g][0] * ROWS
        half = GROUPS[g][1] * ROWS // 2
        for side in range(2):
            near = partial(g, 2 - side)
            far_copy(side, g).wait_recv()
            parts = [near[:half], near[half:]]
            parts[side] = parts[side] + recv_far[side, half_of(g)].astype(F32)
            for i in range(2):
                send_near[side, pl.ds(first + i * half, half)] = parts[i].astype(BF16)
            near_copy(side, g).start()

    def scatter_own(g):
        first, count = GROUPS[g]
        own = partial(g, 0)
        for side in range(2):
            near_copy(side, g).wait_recv()
            own = own + recv_near[side, rows_of(g)].astype(F32)
        sums[pl.ds(first, count)] = own.reshape(count, ROWS, width).astype(BF16)
        if g == 0:
            pltpu.make_async_copy(sums.at[my_core], ret.at[my_core], r_recv.at[0]).start()
        chips = sorted(range(first // CORES, (first + count) // CORES), key=lambda k: -sum(map(abs, CHIPS[k])))
        for k in chips:
            for core in cores(k):
                pltpu.make_async_remote_copy(
                    src_ref=sums.at[k * CORES + core],
                    dst_ref=ret.at[k * CORES + my_core],
                    send_sem=r_send,
                    recv_sem=r_recv.at[g],
                    device_id=device(k, core, -1),
                    device_id_type=MESH,
                ).start()

    pltpu.make_async_copy(pack.at[my_core], xin.at[0, my_core], a_recv.at[0]).start()
    for u in range(3):
        a_start(u)
    gather_first(0)
    a_start(3)
    a_start(4)
    gather_first(1)
    for u in range(5, len(UNITS)):
        a_start(u)
    gather_first(2)

    feature = (mine, left, right, (mine + 2) % tensor_size)
    for j in range(4):
        start = pl.multiple_of(feature[j] * width, width)
        own = pl.ds(j * width, width)
        pltpu.make_async_copy(gate_hbm.at[pl.ds(start, width), :], gate_w.at[own, :], w_sem.at[0]).start()
        pltpu.make_async_copy(up_hbm.at[pl.ds(start, width), :], up_w.at[own, :], w_sem.at[1]).start()
        pltpu.make_async_copy(down_hbm.at[:, pl.ds(start, width)], down_w.at[:, own], w_sem.at[2]).start()

    def weights_here():
        for i, (src, dst) in enumerate(((gate_hbm, gate_w), (up_hbm, up_w), (down_hbm, down_w))):
            pltpu.make_async_copy(src, dst, w_sem.at[i]).wait()

    after = {
        3: (weights_here,),
        5: (lambda: arrived(0, 5), lambda: split_rows(0, range(4)), lambda: forward(0, 0)),
        6: (lambda: forward(0, 1), lambda: scatter_far(0)),
        7: (
            lambda: scatter_near(0), lambda: arrived(5, 7), lambda: split_rows(1, range(4)), lambda: forward(1, 0), lambda: forward(1, 1),
            lambda: scatter_far(1),
        ),
        8: (
            lambda: split_rows(2, range(3)), lambda: forward_part(0), lambda: forward_part(1),
            lambda: scatter_own(0), lambda: scatter_near(1),
        ),
    }
    for u in range(len(UNITS)):
        if u >= 2 and u + 1 < len(UNITS):
            gather_first(u + 1)
        gather_relay(u)
        for task in after.get(u, ()):
            task()
    arrived(7, 9)
    split_rows(2, (3,))
    forward_end(0)
    forward_end(1)
    scatter_far(2)
    scatter_own(1)
    scatter_near(2)
    scatter_own(2)

    place_out.wait()
    others = pl.ds(0, experts - 1)
    pltpu.make_async_copy(pack.at[others], xin.at[0, others], a_send).wait()
    pltpu.make_async_copy(sums.at[others], ret.at[others], r_send).wait()
    for side in range(2):
        relayed = pl.ds(0, experts // 2)
        pltpu.make_async_copy(xin.at[0], xin.at[1 + side], y_send.at[side]).wait()
        pltpu.make_async_copy(xin.at[1 + side, relayed], xin.at[3, relayed], o_send.at[side]).wait()
        pltpu.make_async_copy(send_far.at[side], recv_far.at[side], f_send.at[side]).wait()
        pltpu.make_async_copy(send_near.at[side], recv_near.at[side], n_send.at[side]).wait()
    for g in range(len(GROUPS)):
        at = pl.ds(*GROUPS[g])
        pltpu.make_async_copy(sums.at[at], ret.at[at], r_recv.at[g]).wait()


def per_device(tokens, out_grads, species, expert_table, gate_weight, up_weight, down_weight):
    experts = expert_table.shape[0]
    tensor_size = lax.axis_size("tensor")
    count, width = tokens.shape
    capacity = 2 * (count // tensor_size) // experts
    depth, hidden = gate_weight.shape[1:]
    all_rows = experts * ROWS
    hbm = pl.BlockSpec(memory_space=pl.ANY)
    dma = pltpu.SemaphoreType.DMA
    units, groups = len(UNITS), len(GROUPS)
    returned, place = pl.pallas_call(
        functools.partial(kernel, capacity),
        out_shape=(
            pltpu.VMEM((experts, ROWS, width), BF16),
            jax.ShapeDtypeStruct((1, count), jnp.int32),
        ),
        in_specs=[hbm] * 7,
        out_specs=(pl.BlockSpec(memory_space=pltpu.VMEM), hbm),
        scratch_shapes=[
            pltpu.VMEM((count, width), BF16),
            pltpu.VMEM((count, width), BF16),
            pltpu.VMEM((1, count), jnp.int32),
            pltpu.SMEM((experts,), jnp.int32),
            pltpu.VMEM((1, count), jnp.int32),
            pltpu.VMEM((experts, 2 * ROWS, width), BF16),
            pltpu.VMEM((tensor_size, experts, 2 * ROWS, width), BF16),
            pltpu.VMEM((all_rows, depth), BF16),
            pltpu.VMEM((all_rows, depth), BF16),
            pltpu.VMEM((3, GROUPS[-1][1] * ROWS, hidden), F32),
            pltpu.VMEM((depth, hidden), BF16),
            pltpu.VMEM((depth, hidden), BF16),
            pltpu.VMEM((hidden, depth), BF16),
            pltpu.VMEM((all_rows, hidden), BF16),
            pltpu.VMEM((all_rows, hidden), BF16),
            pltpu.VMEM((2, all_rows // 2, width), BF16),
            pltpu.VMEM((2, all_rows, width), BF16),
            pltpu.VMEM((2, all_rows // 2, width), BF16),
            pltpu.VMEM((2, all_rows, width), BF16),
            pltpu.VMEM((experts, ROWS, width), BF16),
            dma((4,)), dma, dma((3,)), dma, dma((units,)),
            dma((2,)), dma((2, units)), dma((2,)), dma((2, units)),
            dma((2,)), dma((2, groups)), dma((2,)), dma((2, groups)), dma, dma((groups,)),
        ],
        compiler_params=pltpu.CompilerParams(
            collective_id=0, has_side_effects=True, vmem_limit_bytes=56 * 1024 * 1024
        ),
    )(tokens, out_grads, species.reshape(1, count), expert_table, gate_weight[0], up_weight[0], down_weight[0])
    ids = lax.broadcasted_iota(jnp.int32, (count, all_rows), 1)
    chosen = (ids == place.reshape(count, 1)).astype(BF16)
    return jnp.dot(chosen, returned.reshape(all_rows, width), preferred_element_type=F32).astype(BF16)


def solution(mesh):
    placed = (
        P("expert", "tensor"),
        P("expert", "tensor"),
        P("expert", None),
        P(),
        P("expert", None, "tensor"),
        P("expert", None, "tensor"),
        P("expert", "tensor", None),
    )
    return jax.shard_map(
        per_device, mesh=mesh, in_specs=placed, out_specs=P("expert", "tensor"), check_vma=False
    )
```
